128 devices in a mesh: vocab: 32 (over z, y, core), tok: 4 (over x).
Axes of the slice: x: 4, y: 4, z: 4, core: 2. Of those that a mesh axis runs over, the one named last changes fastest.
Arguments:
- teacher_hidden: bfloat16 [512, 8192], P(None, 'tok'), may hold values from -80 to 80
- teacher_head: bfloat16 [8192, 81920], P('tok', 'vocab'), may hold values from -0.0625 to 0.0625
- student_hidden: bfloat16 [512, 3584], replicated, may hold values from -80 to 80
- student_head: bfloat16 [3584, 81920], P(None, ('vocab', 'tok')), may hold values from -0.09375 to 0.09375
- grammar_bits: int32 [512, 5120], P('tok', 'vocab'), may hold values from 0 to 65535
- sampled_ids: int32 [512], replicated, may hold values from 0 to 81919
Outputs:
- distill_loss: float32 [], replicated
- head_grad: bfloat16 [3584, 81920], P(None, ('vocab', 'tok'))
- hidden_grad: float32 [512, 3584], P(('vocab', 'tok'))
The draws below stay inside these ranges and needn't reach their ends.
All inputs are finite; a program needn't handle non-finite values.
Results may differ from the reference program's by a relative error of at most 0.0038.
Values may be sent and summed in bfloat16 or wider, within the bound.
No kernel may reach another device: no remote copies, remote signals or barrier semaphores. Data moves between devices by JAX's collectives and lax.ppermute only.
A program may use at most 128 MiB of HBM per device.

```python
import jax
import jax.numpy as jnp
from jax import lax

DT = 8192
DS = 3584
V = 81920
TOKENS = 512


def scaled_rows(key, row_total, width):
    base = jnp.clip(jax.random.normal(key, (row_total, width), jnp.float32), -4.0, 4.0)
    return (3.0 * base).astype(jnp.bfloat16)


def draw_teacher_hidden(key, part):
    return scaled_rows(jax.random.fold_in(key, 11), TOKENS, DT)


def draw_student_hidden(key, part):
    return scaled_rows(jax.random.fold_in(key, 23), TOKENS, DS)


def place_ends(values, stream_key, low, top_value):
    index_at = [jax.random.randint(jax.random.fold_in(stream_key, axis), (), 0, length) for axis, length in enumerate(values.shape)]
    main_axis = values.shape.index(max(values.shape))
    next_to = index_at[:main_axis] + [(index_at[main_axis] + 1) % values.shape[main_axis]] + index_at[main_axis + 1:]
    return values.at[tuple(index_at)].set(low).at[tuple(next_to)].set(top_value)


def shard_levels(own_key, shape, cuts, low, top_value):
    def one(axis_at, shards_of):
        heights = jax.random.uniform(jax.random.fold_in(jax.random.fold_in(own_key, 6), axis_at), (shards_of,), jnp.float32, low / len(cuts), top_value / len(cuts))
        return jnp.repeat(jnp.exp(heights), shape[axis_at] // shards_of).reshape((-1,) + (1,) * (len(shape) - axis_at - 1))

    loudness = one(*cuts[0])
    for cut in cuts[1:]:
        loudness = loudness * one(*cut)
    return loudness


def centred(stream_key, dims, scale, most, shards=(), kind=jnp.bfloat16):
    values = scale * jax.random.normal(stream_key, dims, jnp.float32)
    if shards:
        values = values * shard_levels(stream_key, dims, shards, -0.22, 0.18)
    return jnp.clip(values, -most, most).astype(kind)


def setup_inputs(seed: int = 0) -> dict:
    keys = jax.random.split(jax.random.key(seed), 7)
    return {
        "teacher_hidden": draw_teacher_hidden(jax.random.fold_in(keys[6], 71), 0),
        "teacher_head": centred(keys[1], (DT, V), DT ** -0.5, 0.0625, ((0, 4), (1, 32))),
        "student_hidden": draw_student_hidden(jax.random.fold_in(keys[6], 71), 0),
        "student_head": centred(keys[3], (DS, V), DS ** -0.5, 0.09375, ((1, 128),)),
        "grammar_bits": place_ends(jax.random.randint(keys[4], (TOKENS, V // 16), 0, 65536), jax.random.fold_in(keys[4], 1), 0, 65535).astype(jnp.int32),
        "sampled_ids": place_ends(jax.random.randint(keys[5], (TOKENS,), 0, V), jax.random.fold_in(keys[5], 1), 0, V - 1).astype(jnp.int32),
    }


sample_weight = 0.5


def admitted(packed, sampled_ids, column_start):
    shifts = jnp.arange(16, dtype=jnp.int32)
    bit_values = jnp.right_shift(packed[:, :, None], shifts[None, None, :]) & 1
    unpacked = bit_values.reshape(packed.shape[0], packed.shape[1] * 16)
    columns = column_start + jnp.arange(unpacked.shape[1], dtype=jnp.int32)
    chosen = columns[None, :] == sampled_ids[:, None]
    return (unpacked == 1) | chosen, chosen


def masked_stats(logits, allowed):
    masked = jnp.where(allowed, logits, -1e30)
    local_max = jnp.max(masked, axis=1)
    local_sum = jnp.sum(jnp.where(allowed, jnp.exp(masked - local_max[:, None]), 0.0), axis=1)
    return local_max, local_sum


def reference(teacher_hidden, teacher_head, student_hidden, student_head, grammar_bits, sampled_ids):
    teacher_logit = jnp.dot(teacher_hidden, teacher_head, preferred_element_type=jnp.float32)
    allowed, chosen = admitted(grammar_bits, sampled_ids, 0)
    teacher_max, teacher_sum = masked_stats(teacher_logit, allowed)
    shifted = teacher_logit - teacher_max[:, None]
    teacher_prob = jnp.where(allowed, jnp.exp(shifted) / teacher_sum[:, None], 0.0).astype(jnp.bfloat16)
    teacher_log = shifted - jnp.log(teacher_sum)[:, None]
    student_logit = jnp.dot(student_hidden, student_head, preferred_element_type=jnp.float32)
    student_max = jnp.max(student_logit, axis=1)
    student_sum = jnp.sum(jnp.exp(student_logit - student_max[:, None]), axis=1)
    student_log = student_logit - student_max[:, None] - jnp.log(student_sum)[:, None]
    prob_wide = teacher_prob.astype(jnp.float32)
    divergence = jnp.sum(jnp.where(allowed, prob_wide * teacher_log, 0.0)) - jnp.sum(prob_wide * student_log)
    picked = jnp.sum(jnp.where(chosen, student_log - teacher_log, 0.0))
    distill_loss = (divergence + sample_weight * picked) / TOKENS
    logit_grad = ((1.0 - sample_weight) * jnp.exp(student_log) - prob_wide
                  + sample_weight * chosen.astype(jnp.float32)).astype(jnp.bfloat16)
    head_grad = lax.dot_general(student_hidden, logit_grad, (((0,), (0,)), ((), ())),
                                preferred_element_type=jnp.float32).astype(jnp.bfloat16)
    hidden_grad = lax.dot_general(logit_grad, student_head, (((1,), (1,)), ((), ())),
                                  preferred_element_type=jnp.float32)
    return (distill_loss, head_grad, hidden_grad)
```

```python
import jax
import jax.numpy as jnp
from jax import lax
from jax.experimental import pallas as pl
from jax.experimental.layout import Layout, with_layout_constraint
from jax.sharding import Mesh
from jax.sharding import PartitionSpec as P

sample_weight = 0.5
every_axis = ("z", "y", "c", "x")
wire = jnp.float16
hidden_scale = 1024.0


def device_of(z, y, c, x):
    return ((z % 4 * 4 + y % 4) * 2 + c % 2) * 4 + x % 4


def shift(value, z=0, y=0, c=0, x=0):
    pairs = [
        (device_of(k, j, i, h), device_of(k + z, j + y, i + c, h + x))
        for k in range(4)
        for j in range(4)
        for i in range(2)
        for h in range(4)
    ]
    return lax.ppermute(value, every_axis, pairs)


def wide(a):
    return a.astype(jnp.float32)


def row_major(a):
    return with_layout_constraint(a, Layout(major_to_minor=tuple(range(a.ndim))))


def head_kernel(hidden_ref, grad_ref, out_ref):
    out_ref[...] = lax.dot_general(
        hidden_ref[...],
        grad_ref[...],
        (((0,), (0,)), ((), ())),
        preferred_element_type=jnp.float32,
    ).astype(out_ref.dtype)


def head_product(hidden, grad):
    tokens, width = hidden.shape
    columns = grad.shape[1]
    step = width // 4
    return pl.pallas_call(
        head_kernel,
        grid=(4,),
        in_specs=[
            pl.BlockSpec((tokens, step), lambda i: (0, i)),
            pl.BlockSpec((tokens, columns), lambda i: (0, 0)),
        ],
        out_specs=pl.BlockSpec((step, columns), lambda i: (i, 0)),
        out_shape=jax.ShapeDtypeStruct((width, columns), jnp.bfloat16),
    )(hidden, grad)


def from_all(row):
    count = lax.axis_size(every_axis)
    return lax.all_to_all(
        jnp.broadcast_to(row[None, :], (count, row.shape[0])), every_axis, 0, 0, tiled=True
    )


def admitted(packed, sampled_ids, column_start):
    words = packed.shape[1]
    columns = words * 16
    word_of = jnp.arange(columns, dtype=jnp.int32) // 16
    bit_of = jnp.arange(columns, dtype=jnp.int32) % 16
    here = word_of[None, :] == jnp.arange(words, dtype=jnp.int32)[:, None]
    low_pick = (here & (bit_of < 8)[None, :]).astype(jnp.bfloat16)
    high_pick = (here & (bit_of >= 8)[None, :]).astype(jnp.bfloat16)
    low = (packed & 255).astype(jnp.bfloat16)
    high = (packed >> 8).astype(jnp.bfloat16)
    byte = jnp.dot(
        jnp.concatenate([low, high], axis=1),
        jnp.concatenate([low_pick, high_pick], axis=0),
        preferred_element_type=jnp.float32,
    ).astype(jnp.int32)
    bit = jnp.right_shift(byte, (bit_of % 8)[None, :]) & 1
    chosen = (column_start + jnp.arange(columns, dtype=jnp.int32))[None, :] == sampled_ids[:, None]
    return ((bit == 1) | chosen, chosen)


def per_device(
    teacher_hidden, teacher_head, student_hidden, student_head, grammar_bits, sampled_ids
):
    x = lax.axis_index("x")
    core = lax.axis_index("c")
    z = lax.axis_index("z")
    column_block = lax.axis_index(every_axis)
    token_total, width = student_hidden.shape
    columns = student_head.shape[1]
    rows = token_total // 2

    def teacher_block(step):
        weights = lax.dynamic_slice_in_dim(teacher_head, (x + step) % 4 * columns, columns, 1)
        return row_major(
            jnp.dot(teacher_hidden, weights, preferred_element_type=jnp.float32)
        )

    far = teacher_block(2).astype(wire)
    far = shift(far, x=2)
    after = teacher_block(1).astype(wire)
    after = shift(after, x=1)
    before = teacher_block(3).astype(wire)
    before = shift(before, x=3)
    own = lax.optimization_barrier(teacher_block(0))
    student_logit = row_major(
        jnp.dot(student_hidden, student_head, preferred_element_type=jnp.float32)
    )
    student_top = jnp.max(student_logit, axis=1)
    student_sum = jnp.sum(jnp.exp(student_logit - student_top[:, None]), axis=1)
    student_lse = student_top + jnp.log(student_sum)
    packed = lax.all_to_all(grammar_bits, "x", split_axis=1, concat_axis=0, tiled=True)
    allowed, chosen = admitted(packed, sampled_ids, column_block * columns)

    teacher_logit = row_major(own + wide(far) + (wide(after) + wide(before)))
    masked = jnp.where(allowed, teacher_logit, -1e30)
    teacher_top = jnp.max(masked, axis=1)
    teacher_sum = jnp.sum(
        jnp.where(allowed, jnp.exp(masked - teacher_top[:, None]), 0.0), axis=1
    )
    teacher_lse = jnp.where(
        teacher_sum > 0.0, teacher_top + jnp.log(jnp.maximum(teacher_sum, 1.0)), -1e30
    )
    block_at = [(z + step) % 4 for step in range(4)]
    early = jnp.stack(block_at + [core, 1 - core] + [core] * 122).astype(jnp.float32)
    every = from_all(jnp.concatenate([teacher_lse, student_lse, early]))[:, : 2 * token_total]
    top = jnp.max(every, axis=0)
    lse = top + jnp.log(jnp.sum(jnp.exp(every - top[None, :]), axis=0))
    teacher_log = teacher_logit - lse[:token_total, None]
    student_log = student_logit - lse[token_total:, None]

    teacher_prob = jnp.where(allowed, jnp.exp(teacher_log), 0.0).astype(jnp.bfloat16)
    prob_wide = wide(teacher_prob)
    logit_grad = row_major(
        (
            (1.0 - sample_weight) * jnp.exp(student_log)
            - prob_wide
            + sample_weight * wide(chosen)
        ).astype(jnp.bfloat16)
    )

    by_core = logit_grad.reshape(16, 2, 16, columns)

    def hidden_rows(which):
        part = lax.dynamic_index_in_dim(by_core, which, 1, False).reshape(rows, columns)
        return hidden_scale * lax.dot_general(
            part, student_head, (((1,), (1,)), ((), ())), preferred_element_type=jnp.float32
        )

    other = hidden_rows(1 - core).astype(wire)
    sent = shift(other, c=1).reshape(4, 64, width)
    mine = lax.optimization_barrier(hidden_rows(core)).reshape(4, 64, width)

    def block(step):
        index = block_at[step]
        return lax.dynamic_index_in_dim(mine, index, 0, False) + wide(
            lax.dynamic_index_in_dim(sent, index, 0, False)
        )

    up = shift(block(1).astype(wire), z=1)
    down = shift(block(3).astype(wire), z=3)
    across = shift(block(2).astype(wire), z=2)
    mine = block(0) + (wide(up) + wide(down)) + wide(across)

    head_grad = head_product(student_hidden, logit_grad)
    gap = teacher_log - student_log
    loss_part = jnp.sum(prob_wide * gap) - sample_weight * jnp.sum(jnp.where(chosen, gap, 0.0))
    losses = from_all(jnp.broadcast_to(loss_part, (128,)))
    distill_loss = jnp.sum(losses[:, 0]) / token_total

    last = lax.all_to_all(mine.astype(wire).reshape(16, 4, width), ("y", "x"), 0, 0, tiled=True)
    hidden_grad = jnp.sum(wide(last), axis=0) * (1.0 / hidden_scale)
    return (distill_loss, head_grad, hidden_grad)


def solution(mesh):
    split = Mesh(mesh.devices.reshape(4, 4, 2, 4), every_axis)
    vocab = ("z", "y", "c")
    placed = (
        P(None, "x"),
        P("x", vocab),
        P(),
        P(None, every_axis),
        P("x", vocab),
        P(),
    )
    return jax.shard_map(
        per_device,
        mesh=split,
        in_specs=placed,
        out_specs=(P(), P(None, every_axis), P(every_axis, None)),
        check_vma=False,
    )
```

```python
import jax
import jax.numpy as jnp
from jax import lax
from jax.experimental import pallas as pl
from jax.experimental.layout import Layout, with_layout_constraint
from jax.sharding import Mesh
from jax.sharding import PartitionSpec as P

sample_weight = 0.5
every_axis = ("z", "y", "c", "x")
wire = jnp.float16
hidden_scale = 1024.0


def device_of(z, y, c, x):
    return ((z % 4 * 4 + y % 4) * 2 + c % 2) * 4 + x % 4


def shift(value, z=0, y=0, c=0, x=0):
    pairs = [
        (device_of(k, j, i, h), device_of(k + z, j + y, i + c, h + x))
        for k in range(4)
        for j in range(4)
        for i in range(2)
        for h in range(4)
    ]
    return lax.ppermute(value, every_axis, pairs)


def swap(value, z=0, y=0, c=0, x=0):
    pairs = [
        (device_of(k, j, i, h), device_of(k ^ z, j ^ y, i ^ c, h ^ x))
        for k in range(4)
        for j in range(4)
        for i in range(2)
        for h in range(4)
    ]
    return lax.ppermute(value, every_axis, pairs)


def core_shift(value, step):
    pairs = [
        (
            device_of(k, j, i, h),
            device_of(k, j + step, i, h) if i == 0 else device_of(k + step, j, i, h),
        )
        for k in range(4)
        for j in range(4)
        for i in range(2)
        for h in range(4)
    ]
    return lax.ppermute(value, every_axis, pairs)


plane_groups = [
    [device_of(k, j, 0, h) for k in range(4) for h in range(4)] for j in range(4)
] + [[device_of(k, j, 1, h) for j in range(4) for h in range(4)] for k in range(4)]


def merged(parts):
    scores = [part[:8] for part in parts]
    terms = [part[8:] for part in parts]
    top = scores[0]
    for score in scores[1:]:
        top = jnp.maximum(top, score)
    shares = [jnp.exp(score - top) for score in scores]
    while len(shares) > 1:
        shares = [shares[i] + shares[i + 1] for i in range(0, len(shares), 2)]
    total = top + jnp.log(shares[0])
    is_gap = lax.broadcasted_iota(jnp.int32, (8, 128), 0) < 4
    weighed = [
        jnp.where(is_gap, jnp.exp(score - total), 1.0) * term
        for score, term in zip(scores, terms)
    ]
    while len(weighed) > 1:
        weighed = [weighed[i] + weighed[i + 1] for i in range(0, len(weighed), 2)]
    return jnp.concatenate([total, weighed[0]])


def wide(a):
    return a.astype(jnp.float32)


def row_major(a):
    return with_layout_constraint(a, Layout(major_to_minor=tuple(range(a.ndim))))


def head_kernel(hidden_ref, grad_ref, out_ref):
    out_ref[...] = lax.dot_general(
        hidden_ref[...],
        grad_ref[...],
        (((0,), (0,)), ((), ())),
        preferred_element_type=jnp.float32,
    ).astype(out_ref.dtype)


def head_product(hidden, grad):
    tokens, width = hidden.shape
    columns = grad.shape[1]
    step = width // 4
    return pl.pallas_call(
        head_kernel,
        grid=(4,),
        in_specs=[
            pl.BlockSpec((tokens, step), lambda i: (0, i)),
            pl.BlockSpec((tokens, columns), lambda i: (0, 0)),
        ],
        out_specs=pl.BlockSpec((step, columns), lambda i: (i, 0)),
        out_shape=jax.ShapeDtypeStruct((width, columns), jnp.bfloat16),
    )(hidden, grad)


def admitted(packed, sampled_ids, column_start):
    words = packed.shape[1]
    columns = words * 16
    word_of = jnp.arange(columns, dtype=jnp.int32) // 16
    bit_of = jnp.arange(columns, dtype=jnp.int32) % 16
    here = word_of[None, :] == jnp.arange(words, dtype=jnp.int32)[:, None]
    low_pick = (here & (bit_of < 8)[None, :]).astype(jnp.bfloat16)
    high_pick = (here & (bit_of >= 8)[None, :]).astype(jnp.bfloat16)
    low = (packed & 255).astype(jnp.bfloat16)
    high = (packed >> 8).astype(jnp.bfloat16)
    byte = jnp.dot(
        jnp.concatenate([low, high], axis=1),
        jnp.concatenate([low_pick, high_pick], axis=0),
        preferred_element_type=jnp.float32,
    ).astype(jnp.int32)
    bit = jnp.right_shift(byte, (bit_of % 8)[None, :]) & 1
    chosen = (column_start + jnp.arange(columns, dtype=jnp.int32))[None, :] == sampled_ids[:, None]
    return ((bit == 1) | chosen, chosen)


def per_device(
    teacher_hidden, teacher_head, student_hidden, student_head, grammar_bits, sampled_ids
):
    x = lax.axis_index("x")
    core = lax.axis_index("c")
    place = jnp.where(core == 0, lax.axis_index("y"), lax.axis_index("z"))
    column_block = lax.axis_index(every_axis)
    token_total, width = student_hidden.shape
    columns = student_head.shape[1]
    rows = token_total // 2

    def teacher_block(step):
        weights = lax.dynamic_slice_in_dim(teacher_head, (x + step) % 4 * columns, columns, 1)
        return row_major(
            jnp.dot(teacher_hidden, weights, preferred_element_type=jnp.float32)
        )

    far = teacher_block(2).astype(wire)
    far = shift(far, x=2)
    after = teacher_block(1).astype(wire)
    after = shift(after, x=1)
    before = teacher_block(3).astype(wire)
    before = shift(before, x=3)
    own = lax.optimization_barrier(teacher_block(0))
    student_logit = row_major(
        jnp.dot(student_hidden, student_head, preferred_element_type=jnp.float32)
    )
    student_top = jnp.max(student_logit, axis=1)
    student_sum = jnp.sum(jnp.exp(student_logit - student_top[:, None]), axis=1)
    student_lse = student_top + jnp.log(student_sum)
    packed = lax.all_to_all(grammar_bits, "x", split_axis=1, concat_axis=0, tiled=True)
    allowed, chosen = admitted(packed, sampled_ids, column_block * columns)

    teacher_logit = row_major(own + wide(far) + (wide(after) + wide(before)))
    masked = jnp.where(allowed, teacher_logit, -1e30)
    teacher_top = jnp.max(masked, axis=1)
    weight = jnp.where(allowed, jnp.exp(masked - teacher_top[:, None]), 0.0)
    gap = teacher_logit - student_logit
    teacher_sum = jnp.maximum(jnp.sum(weight, axis=1), 1e-30)
    teacher_lse = jnp.maximum(teacher_top + jnp.log(teacher_sum), -1e30)
    gap_mean = jnp.sum(weight * gap, axis=1) / teacher_sum
    picked = jnp.sum(jnp.where(chosen, gap, 0.0), axis=1)
    stats = jnp.concatenate([teacher_lse, student_lse, gap_mean, picked]).reshape(16, 128)
    stats = merged([stats, swap(stats, c=1)])
    for axis in ("x", "y", "z"):
        far_stats = swap(stats, **{axis: 2})
        near_stats = swap(stats, **{axis: 1})
        next_stats = swap(stats, **{axis: 3})
        stats = merged([stats, far_stats, near_stats, next_stats])
    lse = stats[:8].reshape(2 * token_total)
    apart = stats[4:8] - stats[:4]
    distill_loss = (
        jnp.sum(stats[8:12] + (1.0 - sample_weight) * apart - sample_weight * stats[12:])
        / token_total
    )
    teacher_log = teacher_logit - lse[:token_total, None]
    student_log = student_logit - lse[token_total:, None]

    teacher_prob = jnp.where(allowed, jnp.exp(teacher_log), 0.0).astype(jnp.bfloat16)
    prob_wide = wide(teacher_prob)
    logit_grad = row_major(
        (
            (1.0 - sample_weight) * jnp.exp(student_log)
            - prob_wide
            + sample_weight * wide(chosen)
        ).astype(jnp.bfloat16)
    )

    by_core = logit_grad.reshape(16, 2, 16, columns)

    def hidden_rows(which):
        part = lax.dynamic_index_in_dim(by_core, which, 1, False).reshape(4, 4, 16, columns)
        part = jnp.where(which == 0, part.swapaxes(0, 1), part).reshape(rows, columns)
        return hidden_scale * lax.dot_general(
            part, student_head, (((1,), (1,)), ((), ())), preferred_element_type=jnp.float32
        )

    other = hidden_rows(1 - core).astype(wire)
    sent = shift(other, c=1).reshape(4, 64, width)
    mine = lax.optimization_barrier(hidden_rows(core)).reshape(4, 64, width)

    def block(step):
        index = (place + step) % 4
        return lax.dynamic_index_in_dim(mine, index, 0, False) + wide(
            lax.dynamic_index_in_dim(sent, index, 0, False)
        )

    up = core_shift(block(1).astype(wire), 1)
    down = core_shift(block(3).astype(wire), 3)
    across = core_shift(block(2).astype(wire), 2)
    mine = block(0) + (wide(up) + wide(down)) + wide(across)

    head_grad = head_product(student_hidden, logit_grad)
    last = lax.all_to_all(
        mine.astype(wire).reshape(16, 4, width),
        every_axis,
        0,
        0,
        axis_index_groups=plane_groups,
        tiled=True,
    )
    hidden_grad = jnp.sum(wide(last), axis=0) * (1.0 / hidden_scale)
    return (distill_loss, head_grad, hidden_grad)


def solution(mesh):
    split = Mesh(mesh.devices.reshape(4, 4, 2, 4), every_axis)
    vocab = ("z", "y", "c")
    placed = (
        P(None, "x"),
        P("x", vocab),
        P(),
        P(None, every_axis),
        P("x", vocab),
        P(),
    )
    return jax.shard_map(
        per_device,
        mesh=split,
        in_specs=placed,
        out_specs=(P(), P(None, every_axis), P(every_axis, None)),
        check_vma=False,
    )
```

```python
import jax
import jax.numpy as jnp
from jax import lax
from jax.experimental import pallas as pl
from jax.experimental.layout import Layout, with_layout_constraint
from jax.sharding import Mesh
from jax.sharding import PartitionSpec as P

sample_weight = 0.5
every_axis = ("z", "y", "c", "x")
wire = jnp.float16
hidden_scale = 1024.0


def device_of(z, y, c, x):
    return ((z % 4 * 4 + y % 4) * 2 + c % 2) * 4 + x % 4


def shift(value, z=0, y=0, c=0, x=0):
    pairs = [
        (device_of(k, j, i, h), device_of(k + z, j + y, i + c, h + x))
        for k in range(4)
        for j in range(4)
        for i in range(2)
        for h in range(4)
    ]
    return lax.ppermute(value, every_axis, pairs)


def swap(value, z=0, y=0, c=0, x=0):
    pairs = [
        (device_of(k, j, i, h), device_of(k ^ z, j ^ y, i ^ c, h ^ x))
        for k in range(4)
        for j in range(4)
        for i in range(2)
        for h in range(4)
    ]
    return lax.ppermute(value, every_axis, pairs)


def core_shift(value, step):
    pairs = [
        (
            device_of(k, j, i, h),
            device_of(k, j + step, i, h) if i == 0 else device_of(k + step, j, i, h),
        )
        for k in range(4)
        for j in range(4)
        for i in range(2)
        for h in range(4)
    ]
    return lax.ppermute(value, every_axis, pairs)


plane_groups = [
    [device_of(k, j, 0, h) for k in range(4) for h in range(4)] for j in range(4)
] + [[device_of(k, j, 1, h) for j in range(4) for h in range(4)] for k in range(4)]


def merged(parts):
    scores = [part[:8] for part in parts]
    terms = [part[8:] for part in parts]
    top = scores[0]
    for score in scores[1:]:
        top = jnp.maximum(top, score)
    shares = [jnp.exp(score - top) for score in scores]
    while len(shares) > 1:
        shares = [shares[i] + shares[i + 1] for i in range(0, len(shares), 2)]
    total = top + jnp.log(shares[0])
    is_gap = lax.broadcasted_iota(jnp.int32, (8, 128), 0) < 4
    weighed = [
        jnp.where(is_gap, jnp.exp(score - total), 1.0) * term
        for score, term in zip(scores, terms)
    ]
    while len(weighed) > 1:
        weighed = [weighed[i] + weighed[i + 1] for i in range(0, len(weighed), 2)]
    return jnp.concatenate([total, weighed[0]])


def wide(a):
    return a.astype(jnp.float32)


def row_major(a):
    return with_layout_constraint(a, Layout(major_to_minor=tuple(range(a.ndim))))


def head_kernel(hidden_ref, grad_ref, out_ref):
    out_ref[...] = lax.dot_general(
        hidden_ref[...],
        grad_ref[...],
        (((0,), (0,)), ((), ())),
        preferred_element_type=jnp.float32,
    ).astype(out_ref.dtype)


def head_product(hidden, grad):
    tokens, width = hidden.shape
    columns = grad.shape[1]
    step = width // 4
    return pl.pallas_call(
        head_kernel,
        grid=(4,),
        in_specs=[
            pl.BlockSpec((tokens, step), lambda i: (0, i)),
            pl.BlockSpec((tokens, columns), lambda i: (0, 0)),
        ],
        out_specs=pl.BlockSpec((step, columns), lambda i: (i, 0)),
        out_shape=jax.ShapeDtypeStruct((width, columns), jnp.bfloat16),
    )(hidden, grad)


def admitted(packed, sampled_ids, column_start):
    words = packed.shape[1]
    columns = words * 16
    word_of = jnp.arange(columns, dtype=jnp.int32) // 16
    bit_of = jnp.arange(columns, dtype=jnp.int32) % 16
    here = word_of[None, :] == jnp.arange(words, dtype=jnp.int32)[:, None]
    low_pick = (here & (bit_of < 8)[None, :]).astype(jnp.bfloat16)
    high_pick = (here & (bit_of >= 8)[None, :]).astype(jnp.bfloat16)
    low = (packed & 255).astype(jnp.bfloat16)
    high = (packed >> 8).astype(jnp.bfloat16)
    byte = jnp.dot(
        jnp.concatenate([low, high], axis=1),
        jnp.concatenate([low_pick, high_pick], axis=0),
        preferred_element_type=jnp.float32,
    ).astype(jnp.int32)
    bit = jnp.right_shift(byte, (bit_of % 8)[None, :]) & 1
    chosen = (column_start + jnp.arange(columns, dtype=jnp.int32))[None, :] == sampled_ids[:, None]
    return ((bit == 1) | chosen, chosen)


def per_device(
    teacher_hidden, teacher_head, student_hidden, student_head, grammar_bits, sampled_ids
):
    x = lax.axis_index("x")
    core = lax.axis_index("c")
    place = jnp.where(core == 0, lax.axis_index("y"), lax.axis_index("z"))
    column_block = lax.axis_index(every_axis)
    token_total, width = student_hidden.shape
    columns = student_head.shape[1]
    rows = token_total // 2

    def teacher_block(step):
        weights = lax.dynamic_slice_in_dim(teacher_head, (x + step) % 4 * columns, columns, 1)
        return row_major(
            jnp.dot(teacher_hidden, weights, preferred_element_type=jnp.float32)
        )

    far = teacher_block(2).astype(wire)
    far = shift(far, x=2)
    after = teacher_block(1).astype(wire)
    after = shift(after, x=1)
    before = teacher_block(3).astype(wire)
    before = shift(before, x=3)
    own = lax.optimization_barrier(teacher_block(0))
    student_logit = row_major(
        jnp.dot(student_hidden, student_head, preferred_element_type=jnp.float32)
    )
    student_top = jnp.max(student_logit, axis=1)
    student_sum = jnp.sum(jnp.exp(student_logit - student_top[:, None]), axis=1)
    student_lse = student_top + jnp.log(student_sum)
    packed = lax.all_to_all(grammar_bits, "x", split_axis=1, concat_axis=0, tiled=True)
    allowed, chosen = admitted(packed, sampled_ids, column_block * columns)

    teacher_logit = row_major(own + wide(far) + (wide(after) + wide(before)))
    masked = jnp.where(allowed, teacher_logit, -1e30)
    teacher_top = jnp.max(masked, axis=1)
    weight = jnp.where(allowed, jnp.exp(masked - teacher_top[:, None]), 0.0)
    gap = teacher_logit - student_logit
    teacher_sum = jnp.maximum(jnp.sum(weight, axis=1), 1e-30)
    teacher_lse = jnp.maximum(teacher_top + jnp.log(teacher_sum), -1e30)
    gap_mean = jnp.sum(weight * gap, axis=1) / teacher_sum
    picked = jnp.sum(jnp.where(chosen, gap, 0.0), axis=1)
    stats = jnp.concatenate([teacher_lse, student_lse, gap_mean, picked]).reshape(16, 128)
    stats = merged([stats, swap(stats, c=1)])
    for axis in ("x",):
        far_stats = swap(stats, **{axis: 2})
        near_stats = swap(stats, **{axis: 1})
        next_stats = swap(stats, **{axis: 3})
        stats = merged([stats, far_stats, near_stats, next_stats])
    every = lax.all_to_all(
        jnp.broadcast_to(stats[None], (16, 16, 128)), ("z", "y"), 0, 0, tiled=True
    )
    top = jnp.max(every[:, :8], axis=0)
    score = top + jnp.log(jnp.sum(jnp.exp(every[:, :8] - top[None]), axis=0))
    is_gap = lax.broadcasted_iota(jnp.int32, (8, 128), 0) < 4
    share = jnp.where(is_gap[None], jnp.exp(every[:, :8] - score[None]), 1.0)
    stats = jnp.concatenate([score, jnp.sum(share * every[:, 8:], axis=0)])
    lse = stats[:8].reshape(2 * token_total)
    apart = stats[4:8] - stats[:4]
    distill_loss = (
        jnp.sum(stats[8:12] + (1.0 - sample_weight) * apart - sample_weight * stats[12:])
        / token_total
    )
    teacher_log = teacher_logit - lse[:token_total, None]
    student_log = student_logit - lse[token_total:, None]

    teacher_prob = jnp.where(allowed, jnp.exp(teacher_log), 0.0).astype(jnp.bfloat16)
    prob_wide = wide(teacher_prob)
    logit_grad = row_major(
        (
            (1.0 - sample_weight) * jnp.exp(student_log)
            - prob_wide
            + sample_weight * wide(chosen)
        ).astype(jnp.bfloat16)
    )

    by_core = logit_grad.reshape(16, 2, 16, columns)

    def hidden_rows(which):
        part = lax.dynamic_index_in_dim(by_core, which, 1, False).reshape(4, 4, 16, columns)
        part = jnp.where(which == 0, part.swapaxes(0, 1), part).reshape(rows, columns)
        return hidden_scale * lax.dot_general(
            part, student_head, (((1,), (1,)), ((), ())), preferred_element_type=jnp.float32
        )

    other = hidden_rows(1 - core).astype(wire)
    sent = shift(other, c=1).reshape(4, 64, width)
    mine = lax.optimization_barrier(hidden_rows(core)).reshape(4, 64, width)

    def block(step):
        index = (place + step) % 4
        return lax.dynamic_index_in_dim(mine, index, 0, False) + wide(
            lax.dynamic_index_in_dim(sent, index, 0, False)
        )

    up = core_shift(block(1).astype(wire), 1)
    down = core_shift(block(3).astype(wire), 3)
    across = core_shift(block(2).astype(wire), 2)
    mine = block(0) + (wide(up) + wide(down)) + wide(across)

    head_grad = head_product(student_hidden, logit_grad)
    last = lax.all_to_all(
        mine.astype(wire).reshape(16, 4, width),
        every_axis,
        0,
        0,
        axis_index_groups=plane_groups,
        tiled=True,
    )
    hidden_grad = jnp.sum(wide(last) * (1.0 / hidden_scale), axis=0)
    return (distill_loss, head_grad, hidden_grad)


def solution(mesh):
    split = Mesh(mesh.devices.reshape(4, 4, 2, 4), every_axis)
    vocab = ("z", "y", "c")
    placed = (
        P(None, "x"),
        P("x", vocab),
        P(),
        P(None, every_axis),
        P("x", vocab),
        P(),
    )
    return jax.shard_map(
        per_device,
        mesh=split,
        in_specs=placed,
        out_specs=(P(), P(None, every_axis), P(every_axis, None)),
        check_vma=False,
    )
```
